128 devices in a mesh: ctx: 8 (over y, core), exp: 16 (over z, x).
Axes of the slice: x: 4, y: 4, z: 4, core: 2. Of those that a mesh axis runs over, the one named last changes fastest.
Arguments:
- hidden: bfloat16 [16, 1024, 4096], P('exp', 'ctx'), may hold values from -6 to 6
- queries: bfloat16 [16, 1024, 4096], P('exp', 'ctx'), may hold values from -4.5 to 4.5
- new_keys: bfloat16 [16, 1024, 512], P('exp', 'ctx'), may hold values from -6 to 6
- new_values: bfloat16 [16, 1024, 512], P('exp', 'ctx'), may hold values from -6 to 6
- cache_keys: bfloat16 [16, 1024, 512], P('exp', 'ctx'), may hold values from -4.5 to 4.5
- cache_values: bfloat16 [16, 1024, 512], P('exp', 'ctx'), may hold values from -6 to 6
- out_weight: bfloat16 [4096, 4096], P(('ctx', 'exp')), may hold values from -1.5 to 1.5
- norm_gain: bfloat16 [4096], replicated, may hold values from 0.099609375 to 1.8984375
- gate_proj: bfloat16 [128, 4096, 768], P(('ctx', 'exp')), may hold values from -0.09375 to 0.09375
- up_proj: bfloat16 [128, 4096, 768], P(('ctx', 'exp')), may hold values from -0.09375 to 0.09375
- down_proj: bfloat16 [128, 768, 4096], P(('ctx', 'exp')), may hold values from -0.21875 to 0.21875
- expert_ids: int32 [16, 1024, 4], P('exp', 'ctx'), may hold values from 0 to 127, all different within a row; in each aligned block of 128 rows (0 to 127, 128 to 255, ..., all dimensions but the last counted through in order) at most 8 rows name the same one
- gate_fixed: int32 [16, 1024, 4], P('exp', 'ctx'), may hold values from 1 to 65535
Outputs:
- after_attention: bfloat16 [16, 1024, 4096], P('exp', 'ctx')
- layer_output: bfloat16 [16, 1024, 4096], P('exp', 'ctx')
The draws below stay inside these ranges and needn't reach their ends.
Inputs may be any that keep to these rules, and one draw needn't show every extreme that they name: `expert_ids`: each row names 4 different experts. Within the rows of one device (aligned blocks of 128 rows, sequences taken in order) no expert is named more than 8 times, and in some blocks one expert is named exactly 8 times.
All inputs are finite; a program needn't handle non-finite values.
Results may differ from the reference program's by a relative error of at most 0.02.
Values may be sent and summed in bfloat16 or wider, within the bound.
A program may use at most 128 MiB of HBM per device.

```python
import math
import jax
import jax.numpy as jnp
import numpy as np
from jax import lax

D = 4096
HQ = 32
KVH = 4
HD = 128
MOE_FF = 768
TOPK = 4
TOK_DEV = 128
SEQS = 16
WINDOW = 1024
CACHE = 1024
EXPERTS = 128
CAP = 8
N_CTX = 8
N_EXP = 16


def draw_queries(key, part):
    base = 1.5 * jax.random.normal(jax.random.fold_in(key, 1), (SEQS, WINDOW, HQ * HD), jnp.float32)
    return jnp.clip(base, -4.5, 4.5).astype(jnp.bfloat16)


def draw_cache_keys(key, part):
    base = jax.random.normal(jax.random.fold_in(key, 4), (SEQS, CACHE, KVH * HD), jnp.float32)
    return jnp.clip(base, -4.5, 4.5).astype(jnp.bfloat16)


def set_ends(result, own_key, low, top_value):
    extent = result.shape
    index_at = [jax.random.randint(jax.random.fold_in(own_key, axis), (), 0, extent[axis]) for axis in range(len(extent))]
    result = result.at[tuple(index_at)].set(low)
    longest = extent.index(max(extent))
    index_at[longest] = (index_at[longest] + 1) % extent[longest]
    return result.at[tuple(index_at)].set(top_value)


def block_levels(rng, dims, cuts, least, largest):
    gain, own = 1.0, jax.random.fold_in(rng, 6)
    for position, parts in cuts:
        heights = jnp.exp(jax.random.uniform(jax.random.fold_in(own, position), (parts,), jnp.float32, least / len(cuts), largest / len(cuts)))
        gain = gain * jnp.repeat(heights, dims[position] // parts).reshape([-1 if axis == position else 1 for axis in range(len(dims))])
    return gain


def routed_block(stream_key, own, number, rows, amount, top, reach, skew):
    sequence = jax.random.permutation(stream_key, amount)
    heavy_load, usual = portions_of(amount, rows * top, reach, skew, True), portions_of(amount, rows * top, reach, skew, False)
    places = jnp.arange(amount)

    def named(sizes, rotation):
        used = int((sizes > 0).sum())
        fixed = max(1, used // 4)
        shifted = fixed + (places - fixed + rotation * (used - fixed)) % max(1, amount - fixed)
        return jnp.zeros((amount,), jnp.int32).at[sequence[jnp.where(places < fixed, places, shifted)]].set(jnp.asarray(sizes, jnp.int32))

    sizes = jnp.where(number % 4 == 0, named(heavy_load, number // 4), named(usual, number - number // 4 - 1))
    mixed = jax.random.permutation(jax.random.fold_in(own, 3), amount)
    giver, sink = mixed[0:amount // 2 * 2:2], mixed[1:amount // 2 * 2:2]
    slack = jnp.minimum(sizes[giver] - 1, reach - sizes[sink]) // 2
    slack = jnp.where((giver == sequence[0]) | (sink == sequence[0]) | (sizes[sink] == 0), 0, jnp.maximum(slack, 0))
    shifted = jax.random.randint(jax.random.fold_in(own, 4), (amount // 2,), 0, 1 << 20) % (slack + 1)
    sizes = sizes.at[giver].add(-shifted).at[sink].add(shifted)
    labels = jnp.searchsorted(jnp.cumsum(sizes), jnp.arange(rows * top), side="right").astype(jnp.int32)
    table = labels.reshape(top, rows).T
    table = table[jax.random.permutation(jax.random.fold_in(own, 1), rows)]
    rotation = jax.random.randint(jax.random.fold_in(own, 2), (rows, 1), 0, top)
    return jnp.take_along_axis(table, (jnp.arange(top)[None, :] + rotation) % top, axis=1)


def portions_of(number_of, total, limit, lean, full):
    loads = [(1 << 20) // math.isqrt(standing ** lean) + 1 for standing in range(1, number_of + 1)]
    largest = limit if full else min(limit, max(-(-total // number_of), total * loads[0] // sum(loads)))
    least = 1 if total - largest >= number_of - 1 else 0
    holding, surplus = [largest] + [least] * (number_of - 1), total - largest - least * (number_of - 1)
    while surplus > 0:
        candidates = [i for i in range(1, number_of) if holding[i] < largest] or [i for i in range(1, number_of) if holding[i] < limit]
        mass, budget = sum([loads[i] for i in candidates]), surplus
        for i in candidates:
            addition = min(limit - holding[i], max(1, budget * loads[i] // mass), surplus)
            holding[i] = holding[i] + addition
            surplus = surplus - addition
    return np.array(holding)


def bell_draw(own_key, shape, deviation, limit, cuts=(), kind=jnp.bfloat16):
    array = deviation * jax.random.normal(own_key, shape, jnp.float32)
    if cuts:
        array = array * block_levels(own_key, shape, cuts, -0.22, 0.18)
    return jnp.clip(array, -limit, limit).astype(kind)


def setup_inputs(seed: int = 0) -> dict:
    keys = jax.random.split(jax.random.key(seed), 14)
    hidden = bell_draw(keys[0], (SEQS, WINDOW, D), 1.0, 6.0, ((0, 16), (1, 8)))
    queries = draw_queries(jax.random.fold_in(keys[13], 71), 0)
    new_keys = bell_draw(keys[2], (SEQS, WINDOW, KVH * HD), 1.0, 6.0, ((0, 16), (1, 8)))
    new_values = bell_draw(keys[3], (SEQS, WINDOW, KVH * HD), 1.0, 6.0, ((0, 16), (1, 8)))
    cache_keys = draw_cache_keys(jax.random.fold_in(keys[13], 71), 0)
    cache_values = bell_draw(keys[5], (SEQS, CACHE, KVH * HD), 1.0, 6.0, ((0, 16), (1, 8)))
    out_weight = bell_draw(keys[6], (HQ * HD, D), 0.25, 1.5, ((0, 128),))
    norm_gain = jnp.clip(1.0 + 0.18 * jax.random.normal(keys[7], (D,), jnp.float32), 0.099609375, 1.8984375).astype(jnp.bfloat16)
    gate_proj = bell_draw(keys[8], (EXPERTS, D, MOE_FF), D ** -0.5, 0.09375, ((0, 128),))
    up_proj = bell_draw(keys[9], (EXPERTS, D, MOE_FF), D ** -0.5, 0.09375, ((0, 128),))
    down_proj = bell_draw(keys[10], (EXPERTS, MOE_FF, D), MOE_FF ** -0.5, 0.21875, ((0, 128),))
    expert_ids_keys = jax.random.split(jax.random.fold_in(keys[11], 1), SEQS * WINDOW // TOK_DEV)
    expert_ids_turns = jax.random.permutation(jax.random.fold_in(keys[11], 3), SEQS * WINDOW // TOK_DEV)
    expert_ids = jax.vmap(lambda own, number: routed_block(jax.random.fold_in(keys[11], 2), own, number, TOK_DEV, EXPERTS, TOPK, CAP, 2))(expert_ids_keys, expert_ids_turns).reshape((SEQS, WINDOW, TOPK))
    gate_fixed = set_ends(jax.random.randint(keys[12], (SEQS, WINDOW, TOPK), 1, 65536), jax.random.fold_in(keys[12], 1), 1, 65535).astype(jnp.int32)
    return {"hidden": hidden, "queries": queries, "new_keys": new_keys, "new_values": new_values, "cache_keys": cache_keys, "cache_values": cache_values, "out_weight": out_weight, "norm_gain": norm_gain, "gate_proj": gate_proj, "up_proj": up_proj, "down_proj": down_proj, "expert_ids": expert_ids, "gate_fixed": gate_fixed}


def attend_sequence(operands):
    query_rows, cached_keys, cached_values, window_keys, window_values = operands
    window = query_rows.shape[0]
    group_size = HQ // KVH
    query_heads = query_rows.reshape(window, HQ, HD).astype(jnp.float32)
    all_keys = jnp.concatenate([cached_keys, window_keys], axis=0).reshape(-1, KVH, HD).astype(jnp.float32)
    all_values = jnp.concatenate([cached_values, window_values], axis=0).reshape(-1, KVH, HD).astype(jnp.float32)
    key_heads = jnp.repeat(all_keys, group_size, axis=1)
    value_heads = jnp.repeat(all_values, group_size, axis=1)
    scores = jnp.einsum('whd,lhd->hwl', query_heads, key_heads) / math.sqrt(HD)
    positions = jnp.arange(key_heads.shape[0])[None, None, :]
    query_pos = CACHE + jnp.arange(window)[None, :, None]
    scores = jnp.where(positions <= query_pos, scores, -jnp.inf)
    highest = lax.optimization_barrier(jnp.max(scores, axis=-1, keepdims=True))
    powers = jnp.exp(scores - highest)
    weights = (powers / lax.optimization_barrier(jnp.sum(powers, axis=-1, keepdims=True))).astype(jnp.bfloat16)
    attended = jnp.einsum('hwl,lhd->whd', weights.astype(jnp.float32), value_heads)
    return attended.astype(jnp.bfloat16).reshape(window, HQ * HD)

def reference(hidden, queries, new_keys, new_values, cache_keys, cache_values, out_weight, norm_gain, gate_proj, up_proj, down_proj, expert_ids, gate_fixed):
    attended = lax.map(attend_sequence, (queries, cache_keys, cache_values, new_keys, new_values))
    rows_all = SEQS * WINDOW
    flat_att = attended.reshape(rows_all, HQ * HD)
    group_width = HQ * HD // N_CTX
    summed = jnp.zeros((rows_all, D), jnp.float32)
    for member in range(N_CTX):
        partial_sum = jnp.dot(flat_att[:, member * group_width:(member + 1) * group_width], out_weight[member * group_width:(member + 1) * group_width], preferred_element_type=jnp.float32).astype(jnp.bfloat16)
        partial_sum = lax.optimization_barrier(partial_sum)
        summed = summed + partial_sum.astype(jnp.float32)
    after_attention = (hidden.reshape(rows_all, D).astype(jnp.float32) + summed).astype(jnp.bfloat16)
    after_float = after_attention.astype(jnp.float32)
    normed = (after_float * lax.rsqrt(lax.optimization_barrier(jnp.mean(after_float * after_float, axis=-1, keepdims=True)) + 1e-06) * norm_gain.astype(jnp.float32)).astype(jnp.bfloat16)
    flat_ids = expert_ids.reshape(-1).astype(jnp.int32)
    sorted_order = jnp.argsort(flat_ids, stable=True).astype(jnp.int32)
    counts = lax.optimization_barrier(jnp.sum((flat_ids[:, None] == jnp.arange(EXPERTS, dtype=jnp.int32)[None, :]).astype(jnp.int32), axis=0)).astype(jnp.int32)
    offsets = (jnp.cumsum(counts) - counts).astype(jnp.int32)
    slot_total = CAP * N_CTX * N_EXP
    padded = jnp.concatenate([sorted_order, jnp.zeros((slot_total,), jnp.int32)])
    gate_share = gate_fixed.reshape(-1).astype(jnp.float32) / 65536.0

    def one_expert(accumulated, operands):
        weight_gate, weight_up, weight_down, offset, number = operands
        chosen = lax.dynamic_slice_in_dim(padded, offset.astype(jnp.int32), slot_total)
        live_slots = jnp.arange(slot_total, dtype=jnp.int32) < number
        token_rows = (chosen // TOPK).astype(jnp.int32)
        scaled = jnp.where(live_slots, gate_share[chosen], jnp.zeros((slot_total,), jnp.float32))
        inputs = normed[token_rows]
        gate_act = jnp.dot(inputs, weight_gate, preferred_element_type=jnp.float32)
        up_act = jnp.dot(inputs, weight_up, preferred_element_type=jnp.float32)
        product = (jax.nn.silu(gate_act) * up_act).astype(jnp.bfloat16)
        output = jnp.dot(product, weight_down, preferred_element_type=jnp.float32).astype(jnp.bfloat16)
        accumulated = accumulated.at[token_rows].add(scaled[:, None] * output.astype(jnp.float32))
        return (accumulated, None)
    expert_sum, _ = lax.scan(one_expert, jnp.zeros((rows_all, D), jnp.float32), (gate_proj, up_proj, down_proj, offsets, counts))
    layer_output = (after_float + expert_sum).astype(jnp.bfloat16)
    return (after_attention.reshape(SEQS, WINDOW, D), layer_output.reshape(SEQS, WINDOW, D))
```

```python
import functools
import math

import jax
import jax.numpy as jnp
from jax import lax
from jax.experimental import pallas as pl
from jax.experimental.pallas import tpu as pltpu
from jax.sharding import PartitionSpec as P

D = 4096
KVH = 4
HD = 128
TOPK = 4
CAP = 8


def attention_kernel(blocks, heads, width, buf_ref, out_ref, keys, values):
    rows = buf_ref.shape[1]
    base = heads * HD
    span = blocks * rows

    def load(j, _):
        at = pl.multiple_of(j * rows, rows)
        keys[pl.ds(at, rows), :] = buf_ref[j, :, base : base + HD]
        keys[pl.ds(span + at, rows), :] = buf_ref[j, :, base + HD : base + 2 * HD]
        values[pl.ds(at, rows), :HD] = buf_ref[j, :, base + 2 * HD : base + 3 * HD]
        values[pl.ds(span + at, rows), :HD] = buf_ref[j, :, base + 3 * HD : base + 4 * HD]
        return 0

    lax.fori_loop(0, blocks, load, 0)
    values[:, HD:] = jnp.ones((2 * span, HD), jnp.bfloat16)
    scale = math.log2(math.e) / math.sqrt(HD)
    many = heads * rows

    def block(i, _):
        query = jnp.concatenate(
            [buf_ref[i, :, h * HD : (h + 1) * HD] for h in range(heads)], axis=0
        )
        chunks = span // width + (i * rows) // width + 1

        def chunk(k, carry, masked):
            best, total = carry
            at = pl.multiple_of(k * width, width)
            scores = lax.dot_general(
                query,
                keys[pl.ds(at, width), :],
                (((1,), (1,)), ((), ())),
                preferred_element_type=jnp.float32,
            )
            if masked:
                row = lax.broadcasted_iota(jnp.int32, (many, width), 0) % rows
                col = lax.broadcasted_iota(jnp.int32, (many, width), 1)
                scores = jnp.where(at + col <= span + i * rows + row, scores, -1e30)
            highest = jnp.maximum(best, jnp.max(scores, axis=1, keepdims=True))
            powers = jnp.exp2((scores - highest) * scale).astype(jnp.bfloat16)
            fade = jnp.exp2((best - highest) * scale)
            total = total * fade + jnp.dot(
                powers, values[pl.ds(at, width), :], preferred_element_type=jnp.float32
            )
            return highest, total

        carry = (jnp.full((many, 1), -1e30, jnp.float32), jnp.zeros((many, 2 * HD), jnp.float32))
        carry = lax.fori_loop(0, chunks - 1, functools.partial(chunk, masked=False), carry)
        _, total = chunk(chunks - 1, carry, True)
        result = (total[:, :HD] / total[:, HD:]).astype(jnp.bfloat16)
        at = pl.multiple_of(i * rows, rows)
        for h in range(heads):
            out_ref[pl.ds(at, rows), h * HD : (h + 1) * HD] = result[h * rows : (h + 1) * rows]
        return 0

    lax.fori_loop(0, blocks, block, 0)


def attention(buf, heads):
    blocks, rows, _ = buf.shape
    return pl.pallas_call(
        functools.partial(attention_kernel, blocks, heads, min(512, blocks * rows)),
        out_shape=jax.ShapeDtypeStruct((blocks * rows, heads * HD), jnp.bfloat16),
        in_specs=[pl.BlockSpec(memory_space=pltpu.VMEM)],
        out_specs=pl.BlockSpec(memory_space=pltpu.VMEM),
        scratch_shapes=[
            pltpu.VMEM((2 * blocks * rows, HD), jnp.bfloat16),
            pltpu.VMEM((2 * blocks * rows, 2 * HD), jnp.bfloat16),
        ],
        compiler_params=pltpu.CompilerParams(vmem_limit_bytes=32 * 2**20),
        name="attention",
    )(buf)


def per_device(
    hidden,
    queries,
    new_keys,
    new_values,
    cache_keys,
    cache_values,
    out_weight,
    norm_gain,
    gate_proj,
    up_proj,
    down_proj,
    expert_ids,
    gate_fixed,
):
    context = lax.axis_size("ctx")
    experts = context * lax.axis_size("exp")
    rows = hidden.shape[1]
    copies = context // KVH
    heads = queries.shape[2] // HD // context

    def split(array, parts):
        return jnp.swapaxes(array.reshape(rows, parts, -1), 0, 1)

    kv = jnp.concatenate(
        [split(a[0], KVH) for a in (cache_keys, new_keys, cache_values, new_values)], axis=2
    )
    packed = jnp.concatenate([split(queries[0], context), jnp.repeat(kv, copies, axis=0)], axis=2)
    received = lax.all_to_all(packed, "ctx", split_axis=0, concat_axis=0, tiled=True)
    attended = attention(received, heads)
    proj_rows = lax.all_gather(out_weight, "exp", axis=0, tiled=True)
    projected = lax.psum_scatter(
        jnp.dot(attended, proj_rows, preferred_element_type=jnp.float32).astype(jnp.bfloat16),
        "ctx",
        scatter_dimension=0,
        tiled=True,
    ).astype(jnp.float32)
    after_attention = (hidden[0].astype(jnp.float32) + projected).astype(jnp.bfloat16)
    after_float = after_attention.astype(jnp.float32)
    normed = (
        after_float
        * lax.rsqrt(jnp.mean(after_float * after_float, axis=-1, keepdims=True) + 1e-06)
        * norm_gain.astype(jnp.float32)
    ).astype(jnp.bfloat16)

    flat_ids = expert_ids[0].reshape(-1)
    one_hot = (flat_ids[:, None] == jnp.arange(experts, dtype=jnp.int32)[None, :]).astype(jnp.int32)
    earlier = jnp.cumsum(one_hot, axis=0) - one_hot
    target = flat_ids * CAP + jnp.sum(earlier * one_hot, axis=1)
    slots = experts * CAP
    hits = target.reshape(rows, TOPK)[:, :, None] == jnp.arange(slots, dtype=jnp.int32)
    shares = gate_fixed[0][:, :, None]
    high = jnp.sum(jnp.where(hits, shares // 256, 0), axis=1).astype(jnp.bfloat16)
    low = jnp.sum(jnp.where(hits, shares % 256, 0), axis=1).astype(jnp.bfloat16)
    pick = jnp.any(hits, axis=1).astype(jnp.bfloat16)

    half = D // 2
    exchange = functools.partial(
        lax.all_to_all, axis_name=("ctx", "exp"), split_axis=0, concat_axis=0, tiled=True
    )

    def send(columns):
        rows_out = lax.dot_general(
            pick, columns, (((0,), (0,)), ((), ())), preferred_element_type=jnp.float32
        ).astype(jnp.bfloat16)
        return exchange(rows_out.reshape(experts, CAP, half)).reshape(slots, half)

    first, second = send(normed[:, :half]), send(normed[:, half:])

    def hidden_units(weight):
        return jnp.dot(first, weight[:half], preferred_element_type=jnp.float32) + jnp.dot(
            second, weight[half:], preferred_element_type=jnp.float32
        )

    act = (jax.nn.silu(hidden_units(gate_proj[0])) * hidden_units(up_proj[0])).astype(jnp.bfloat16)

    def give_back(weight):
        out = jnp.dot(act, weight, preferred_element_type=jnp.float32).astype(jnp.bfloat16)
        back = exchange(out.reshape(experts, CAP, half)).reshape(slots, half)
        return jnp.dot(high, back, preferred_element_type=jnp.float32) * (1 / 256) + jnp.dot(
            low, back, preferred_element_type=jnp.float32
        ) * (1 / 65536)

    expert_sum = jnp.concatenate(
        [give_back(down_proj[0][:, :half]), give_back(down_proj[0][:, half:])], axis=1
    )
    layer_output = (after_float + expert_sum).astype(jnp.bfloat16)
    return (after_attention[None], layer_output[None])


def solution(mesh):
    tokens = P("exp", "ctx", None)
    experts = P(("ctx", "exp"), None, None)
    return jax.shard_map(
        per_device,
        mesh=mesh,
        in_specs=(tokens,) * 6
        + (P(("ctx", "exp"), None), P(), experts, experts, experts, tokens, tokens),
        out_specs=(tokens, tokens),
        check_vma=False,
    )
```

```python
import functools
import math

import jax
import jax.numpy as jnp
from jax import lax
from jax.experimental import pallas as pl
from jax.experimental.pallas import tpu as pltpu
from jax.sharding import PartitionSpec as P

D = 4096
KVH = 4
HD = 128
TOPK = 4
CAP = 8
PARTS = 2


def attention_kernel(blocks, heads, width, buf_ref, out_ref, keys, values):
    rows = buf_ref.shape[1]
    base = heads * HD
    span = blocks * rows

    def load(j, _):
        at = pl.multiple_of(j * rows, rows)
        keys[pl.ds(at, rows), :] = buf_ref[j, :, base : base + HD]
        keys[pl.ds(span + at, rows), :] = buf_ref[j, :, base + HD : base + 2 * HD]
        values[pl.ds(at, rows), :HD] = buf_ref[j, :, base + 2 * HD : base + 3 * HD]
        values[pl.ds(span + at, rows), :HD] = buf_ref[j, :, base + 3 * HD : base + 4 * HD]
        return 0

    lax.fori_loop(0, blocks, load, 0)
    values[:, HD:] = jnp.ones((2 * span, HD), jnp.bfloat16)
    scale = math.log2(math.e) / math.sqrt(HD)
    many = heads * rows

    def block(i, _):
        query = jnp.concatenate(
            [buf_ref[i, :, h * HD : (h + 1) * HD] for h in range(heads)], axis=0
        )
        chunks = span // width + (i * rows) // width + 1

        def chunk(k, carry, masked):
            best, total = carry
            at = pl.multiple_of(k * width, width)
            scores = lax.dot_general(
                query,
                keys[pl.ds(at, width), :],
                (((1,), (1,)), ((), ())),
                preferred_element_type=jnp.float32,
            )
            if masked:
                row = lax.broadcasted_iota(jnp.int32, (many, width), 0) % rows
                col = lax.broadcasted_iota(jnp.int32, (many, width), 1)
                scores = jnp.where(at + col <= span + i * rows + row, scores, -1e30)
            highest = jnp.maximum(best, jnp.max(scores, axis=1, keepdims=True))
            powers = jnp.exp2((scores - highest) * scale).astype(jnp.bfloat16)
            fade = jnp.exp2((best - highest) * scale)
            total = total * fade + jnp.dot(
                powers, values[pl.ds(at, width), :], preferred_element_type=jnp.float32
            )
            return highest, total

        carry = (jnp.full((many, 1), -1e30, jnp.float32), jnp.zeros((many, 2 * HD), jnp.float32))
        carry = lax.fori_loop(0, chunks - 1, functools.partial(chunk, masked=False), carry)
        _, total = chunk(chunks - 1, carry, True)
        result = (total[:, :HD] / total[:, HD:]).astype(jnp.bfloat16)
        at = pl.multiple_of(i * rows, rows)
        for h in range(heads):
            out_ref[pl.ds(at, rows), h * HD : (h + 1) * HD] = result[h * rows : (h + 1) * rows]
        return 0

    lax.fori_loop(0, blocks, block, 0)


def attention(buf, heads):
    blocks, rows, _ = buf.shape
    return pl.pallas_call(
        functools.partial(attention_kernel, blocks, heads, min(512, blocks * rows)),
        out_shape=jax.ShapeDtypeStruct((blocks * rows, heads * HD), jnp.bfloat16),
        in_specs=[pl.BlockSpec(memory_space=pltpu.VMEM)],
        out_specs=pl.BlockSpec(memory_space=pltpu.VMEM),
        scratch_shapes=[
            pltpu.VMEM((2 * blocks * rows, HD), jnp.bfloat16),
            pltpu.VMEM((2 * blocks * rows, 2 * HD), jnp.bfloat16),
        ],
        compiler_params=pltpu.CompilerParams(vmem_limit_bytes=32 * 2**20),
        name="attention",
    )(buf)


def retile_kernel(split, x_ref, out_ref):
    half = D // 2
    x = x_ref[...].astype(jnp.float32)
    if split:
        one, two = (x[:, at : at + half].reshape(-1, CAP, half) for at in (0, half))
    else:
        pairs = x.reshape(-1, 2 * CAP, half)
        one, two = pairs[:, :CAP], pairs[:, CAP:]
    upper = lax.broadcasted_iota(jnp.int32, one.shape, 1) < CAP // 2
    if split:
        first = jnp.where(upper, one, pltpu.roll(two, CAP // 2, 1))
        second = jnp.where(upper, pltpu.roll(one, CAP // 2, 1), two)
        out = jnp.concatenate([first, second], axis=1).reshape(-1, half)
        out_ref[...] = out.astype(jnp.bfloat16)
    else:
        first = jnp.where(upper, one, pltpu.roll(two, CAP // 2, 1))
        second = jnp.where(upper, pltpu.roll(one, CAP // 2, 1), two)
        out_ref[:, :half] = first.reshape(-1, half).astype(jnp.bfloat16)
        out_ref[:, half:] = second.reshape(-1, half).astype(jnp.bfloat16)


def retile(x, split):
    rows, columns = x.shape
    shape = (rows * 2, columns // 2) if split else (rows // 2, columns * 2)
    steps = math.gcd(8, max(rows, shape[0]) // (2 * CAP))
    return pl.pallas_call(
        functools.partial(retile_kernel, split),
        grid=(steps,),
        out_shape=jax.ShapeDtypeStruct(shape, jnp.bfloat16),
        in_specs=[pl.BlockSpec((rows // steps, columns), lambda i: (i, 0))],
        out_specs=pl.BlockSpec((shape[0] // steps, shape[1]), lambda i: (i, 0)),
        compiler_params=pltpu.CompilerParams(vmem_limit_bytes=24 * 2**20),
        cost_estimate=pl.CostEstimate(
            flops=4 * rows * columns, transcendentals=0, bytes_accessed=4 * rows * columns
        ),
        name="retile_split" if split else "retile_join",
    )(x)


def per_device(
    hidden,
    queries,
    new_keys,
    new_values,
    cache_keys,
    cache_values,
    out_weight,
    norm_gain,
    gate_proj,
    up_proj,
    down_proj,
    expert_ids,
    gate_fixed,
):
    context = lax.axis_size("ctx")
    experts = context * lax.axis_size("exp")
    rows = hidden.shape[1]
    copies = context // KVH
    heads = queries.shape[2] // HD // context

    def split(array, parts):
        return jnp.swapaxes(array.reshape(rows, parts, -1), 0, 1)

    kv = jnp.concatenate(
        [split(a[0], KVH) for a in (cache_keys, new_keys, cache_values, new_values)], axis=2
    )
    packed = jnp.concatenate([split(queries[0], context), jnp.repeat(kv, copies, axis=0)], axis=2)
    received = lax.all_to_all(packed, "ctx", split_axis=0, concat_axis=0, tiled=True)
    attended = attention(received, heads)
    proj_rows = lax.all_gather(out_weight, "exp", axis=0, tiled=True)
    projected = lax.psum_scatter(
        jnp.dot(attended, proj_rows, preferred_element_type=jnp.float32).astype(jnp.bfloat16),
        "ctx",
        scatter_dimension=0,
        tiled=True,
    ).astype(jnp.float32)
    after_attention = (hidden[0].astype(jnp.float32) + projected).astype(jnp.bfloat16)
    after_float = after_attention.astype(jnp.float32)
    normed = (
        after_float
        * lax.rsqrt(jnp.mean(after_float * after_float, axis=-1, keepdims=True) + 1e-06)
        * norm_gain.astype(jnp.float32)
    ).astype(jnp.bfloat16)

    flat_ids = expert_ids[0].reshape(-1)
    one_hot = (flat_ids[:, None] == jnp.arange(experts, dtype=jnp.int32)[None, :]).astype(jnp.int32)
    earlier = jnp.cumsum(one_hot, axis=0) - one_hot
    rank = jnp.sum(earlier * one_hot, axis=1)
    target = (flat_ids * CAP + rank).reshape(rows, TOPK)
    depth = CAP // 2
    slots = experts * CAP
    half = D // 2
    exchange = functools.partial(
        lax.all_to_all, axis_name=("ctx", "exp"), split_axis=0, concat_axis=0, tiled=True
    )
    place = jnp.arange(slots, dtype=jnp.int32)
    left = (place % CAP < depth)[None]
    shares = gate_fixed[0][:, :, None]

    def two_sides(array):
        zero = jnp.zeros_like(array)
        return jnp.concatenate([jnp.where(left, array, zero), jnp.where(left, zero, array)], axis=0)

    def routing(part):
        hits = target[:, :, None] == place // CAP * CAP + part * depth + place % depth
        high = jnp.sum(jnp.where(hits, shares // 256, 0), axis=1)
        low = jnp.sum(jnp.where(hits, shares % 256, 0), axis=1)
        pick = jnp.any(hits, axis=1).astype(jnp.bfloat16)
        gates = jnp.concatenate([high, low], axis=0).astype(jnp.bfloat16)
        return two_sides(pick), two_sides(gates)

    def send(pick):
        sides = jnp.concatenate([normed[:, :half], normed[:, half:]], axis=0)
        rows_out = lax.dot_general(
            pick, sides, (((0,), (0,)), ((), ())), preferred_element_type=jnp.float32
        ).astype(jnp.bfloat16)
        return exchange(rows_out.reshape(experts, CAP, half)).reshape(slots, half)

    def expert(arrived):
        tokens = retile(arrived, False)
        gate = jnp.dot(tokens, gate_proj[0], preferred_element_type=jnp.float32)
        up = jnp.dot(tokens, up_proj[0], preferred_element_type=jnp.float32)
        act = (jax.nn.silu(gate) * up).astype(jnp.bfloat16)
        out = jnp.dot(act, down_proj[0], preferred_element_type=jnp.float32).astype(jnp.bfloat16)
        tiles = retile(out, True)
        return exchange(tiles.reshape(experts, CAP, half)).reshape(slots, half)

    def combine(gates, back):
        sides = jnp.dot(gates, back, preferred_element_type=jnp.float32).reshape(4, rows, half)
        return jnp.concatenate(
            [sides[at] * (1 / 256) + sides[at + 1] * (1 / 65536) for at in (0, 2)], axis=1
        )

    routes = [routing(part) for part in range(PARTS)]
    arrived = [send(pick) for pick, _ in routes]
    returned = [expert(tokens) for tokens in arrived]
    expert_sum = sum(combine(gates, back) for (_, gates), back in zip(routes, returned))
    layer_output = (after_float + expert_sum).astype(jnp.bfloat16)
    return (after_attention[None], layer_output[None])


def solution(mesh):
    tokens = P("exp", "ctx", None)
    experts = P(("ctx", "exp"), None, None)
    return jax.shard_map(
        per_device,
        mesh=mesh,
        in_specs=(tokens,) * 6
        + (P(("ctx", "exp"), None), P(), experts, experts, experts, tokens, tokens),
        out_specs=(tokens, tokens),
        check_vma=False,
    )
```

```python
import functools
import math

import jax
import jax.numpy as jnp
from jax import lax
from jax.experimental import pallas as pl
from jax.experimental.pallas import tpu as pltpu
from jax.sharding import PartitionSpec as P

D = 4096
KVH = 4
HD = 128
TOPK = 4
CAP = 8
PARTS = 2


def attention_kernel(blocks, heads, width, buf_ref, out_ref, keys, values):
    rows = buf_ref.shape[1]
    base = heads * HD
    span = blocks * rows

    def load(j, _):
        at = pl.multiple_of(j * rows, rows)
        keys[pl.ds(at, rows), :] = buf_ref[j, :, base : base + HD]
        keys[pl.ds(span + at, rows), :] = buf_ref[j, :, base + HD : base + 2 * HD]
        values[pl.ds(at, rows), :HD] = buf_ref[j, :, base + 2 * HD : base + 3 * HD]
        values[pl.ds(span + at, rows), :HD] = buf_ref[j, :, base + 3 * HD : base + 4 * HD]
        return 0

    lax.fori_loop(0, blocks, load, 0)
    values[:, HD:] = jnp.ones((2 * span, HD), jnp.bfloat16)
    scale = math.log2(math.e) / math.sqrt(HD)
    many = heads * rows

    def block(i, _):
        query = jnp.concatenate(
            [buf_ref[i, :, h * HD : (h + 1) * HD] for h in range(heads)], axis=0
        )
        chunks = span // width + (i * rows) // width + 1

        def chunk(k, carry, masked):
            best, total = carry
            at = pl.multiple_of(k * width, width)
            scores = lax.dot_general(
                query,
                keys[pl.ds(at, width), :],
                (((1,), (1,)), ((), ())),
                preferred_element_type=jnp.float32,
            )
            if masked:
                row = lax.broadcasted_iota(jnp.int32, (many, width), 0) % rows
                col = lax.broadcasted_iota(jnp.int32, (many, width), 1)
                scores = jnp.where(at + col <= span + i * rows + row, scores, -1e30)
            highest = jnp.maximum(best, jnp.max(scores, axis=1, keepdims=True))
            powers = jnp.exp2((scores - highest) * scale).astype(jnp.bfloat16)
            fade = jnp.exp2((best - highest) * scale)
            total = total * fade + jnp.dot(
                powers, values[pl.ds(at, width), :], preferred_element_type=jnp.float32
            )
            return highest, total

        carry = (jnp.full((many, 1), -1e30, jnp.float32), jnp.zeros((many, 2 * HD), jnp.float32))
        carry = lax.fori_loop(0, chunks - 1, functools.partial(chunk, masked=False), carry)
        _, total = chunk(chunks - 1, carry, True)
        result = (total[:, :HD] / total[:, HD:]).astype(jnp.bfloat16)
        at = pl.multiple_of(i * rows, rows)
        for h in range(heads):
            out_ref[pl.ds(at, rows), h * HD : (h + 1) * HD] = result[h * rows : (h + 1) * rows]
        return 0

    lax.fori_loop(0, blocks, block, 0)


def attention(buf, heads):
    blocks, rows, _ = buf.shape
    return pl.pallas_call(
        functools.partial(attention_kernel, blocks, heads, min(512, blocks * rows)),
        out_shape=jax.ShapeDtypeStruct((blocks * rows, heads * HD), jnp.bfloat16),
        in_specs=[pl.BlockSpec(memory_space=pltpu.VMEM)],
        out_specs=pl.BlockSpec(memory_space=pltpu.VMEM),
        scratch_shapes=[
            pltpu.VMEM((2 * blocks * rows, HD), jnp.bfloat16),
            pltpu.VMEM((2 * blocks * rows, 2 * HD), jnp.bfloat16),
        ],
        compiler_params=pltpu.CompilerParams(vmem_limit_bytes=32 * 2**20),
        name="attention",
    )(buf)


def retile_kernel(split, x_ref, out_ref):
    half = D // 2
    x = x_ref[...].astype(jnp.float32)
    if split:
        one, two = (x[:, at : at + half].reshape(-1, CAP, half) for at in (0, half))
    else:
        pairs = x.reshape(-1, 2 * CAP, half)
        one, two = pairs[:, :CAP], pairs[:, CAP:]
    upper = lax.broadcasted_iota(jnp.int32, one.shape, 1) < CAP // 2
    if split:
        first = jnp.where(upper, one, pltpu.roll(two, CAP // 2, 1))
        second = jnp.where(upper, pltpu.roll(one, CAP // 2, 1), two)
        out = jnp.concatenate([first, second], axis=1).reshape(-1, half)
        out_ref[...] = out.astype(jnp.bfloat16)
    else:
        first = jnp.where(upper, one, pltpu.roll(two, CAP // 2, 1))
        second = jnp.where(upper, pltpu.roll(one, CAP // 2, 1), two)
        out_ref[:, :half] = first.reshape(-1, half).astype(jnp.bfloat16)
        out_ref[:, half:] = second.reshape(-1, half).astype(jnp.bfloat16)


def retile(x, split):
    rows, columns = x.shape
    shape = (rows * 2, columns // 2) if split else (rows // 2, columns * 2)
    steps = math.gcd(8, max(rows, shape[0]) // (2 * CAP))
    return pl.pallas_call(
        functools.partial(retile_kernel, split),
        grid=(steps,),
        out_shape=jax.ShapeDtypeStruct(shape, jnp.bfloat16),
        in_specs=[pl.BlockSpec((rows // steps, columns), lambda i: (i, 0))],
        out_specs=pl.BlockSpec((shape[0] // steps, shape[1]), lambda i: (i, 0)),
        compiler_params=pltpu.CompilerParams(vmem_limit_bytes=24 * 2**20),
        cost_estimate=pl.CostEstimate(
            flops=4 * rows * columns, transcendentals=0, bytes_accessed=4 * rows * columns
        ),
        name="retile_split" if split else "retile_join",
    )(x)


def pack_kernel(context, q_ref, ck_ref, nk_ref, cv_ref, nv_ref, out_ref):
    base = q_ref.shape[1] // context
    for c in range(context):
        g = c // (context // KVH)
        out_ref[c, :, :base] = q_ref[:, c * base : (c + 1) * base]
        for k, ref in enumerate((ck_ref, nk_ref, cv_ref, nv_ref)):
            at = base + k * HD
            out_ref[c, :, at : at + HD] = ref[:, g * HD : (g + 1) * HD]


def pack(context, *arrays):
    rows, width = arrays[0].shape
    return pl.pallas_call(
        functools.partial(pack_kernel, context),
        out_shape=jax.ShapeDtypeStruct((context, rows, width // context + 4 * HD), jnp.bfloat16),
        in_specs=[pl.BlockSpec(memory_space=pltpu.VMEM)] * len(arrays),
        out_specs=pl.BlockSpec(memory_space=pltpu.VMEM),
        compiler_params=pltpu.CompilerParams(vmem_limit_bytes=16 * 2**20),
        name="pack",
    )(*arrays)


def per_device(
    hidden,
    queries,
    new_keys,
    new_values,
    cache_keys,
    cache_values,
    out_weight,
    norm_gain,
    gate_proj,
    up_proj,
    down_proj,
    expert_ids,
    gate_fixed,
):
    context = lax.axis_size("ctx")
    experts = context * lax.axis_size("exp")
    rows = hidden.shape[1]
    heads = queries.shape[2] // HD // context

    packed = pack(
        context, *(a[0] for a in (queries, cache_keys, new_keys, cache_values, new_values))
    )
    received = lax.all_to_all(packed, "ctx", split_axis=0, concat_axis=0, tiled=True)
    attended = attention(received, heads)
    proj_rows = lax.all_gather(out_weight, "exp", axis=0, tiled=True)
    projected = lax.psum_scatter(
        jnp.dot(attended, proj_rows, preferred_element_type=jnp.float32).astype(jnp.bfloat16),
        "ctx",
        scatter_dimension=0,
        tiled=True,
    ).astype(jnp.float32)
    after_attention = (hidden[0].astype(jnp.float32) + projected).astype(jnp.bfloat16)
    after_float = after_attention.astype(jnp.float32)
    normed = (
        after_float
        * lax.rsqrt(jnp.mean(after_float * after_float, axis=-1, keepdims=True) + 1e-06)
        * norm_gain.astype(jnp.float32)
    ).astype(jnp.bfloat16)

    flat_ids = expert_ids[0].reshape(-1)
    one_hot = (flat_ids[:, None] == jnp.arange(experts, dtype=jnp.int32)[None, :]).astype(jnp.int32)
    earlier = jnp.cumsum(one_hot, axis=0) - one_hot
    rank = jnp.sum(earlier * one_hot, axis=1)
    target = (flat_ids * CAP + rank).reshape(rows, TOPK)
    depth = CAP // 2
    slots = experts * CAP
    half = D // 2
    exchange = functools.partial(
        lax.all_to_all, axis_name=("ctx", "exp"), split_axis=0, concat_axis=0, tiled=True
    )
    place = jnp.arange(slots, dtype=jnp.int32)
    left = (place % CAP < depth)[None]
    shares = gate_fixed[0][:, :, None]

    def two_sides(array):
        zero = jnp.zeros_like(array)
        return jnp.concatenate([jnp.where(left, array, zero), jnp.where(left, zero, array)], axis=0)

    def routing(part):
        hits = target[:, :, None] == place // CAP * CAP + part * depth + place % depth
        high = jnp.sum(jnp.where(hits, shares // 256, 0), axis=1)
        low = jnp.sum(jnp.where(hits, shares % 256, 0), axis=1)
        pick = jnp.any(hits, axis=1).astype(jnp.bfloat16)
        gates = jnp.concatenate([high, low], axis=0).astype(jnp.bfloat16)
        return two_sides(pick), two_sides(gates)

    def send(pick):
        sides = jnp.concatenate([normed[:, :half], normed[:, half:]], axis=0)
        rows_out = lax.dot_general(
            pick, sides, (((0,), (0,)), ((), ())), preferred_element_type=jnp.float32
        ).astype(jnp.bfloat16)
        return exchange(rows_out.reshape(experts, CAP, half)).reshape(slots, half)

    def expert(arrived):
        tokens = retile(arrived, False)
        gate = jnp.dot(tokens, gate_proj[0], preferred_element_type=jnp.float32)
        up = jnp.dot(tokens, up_proj[0], preferred_element_type=jnp.float32)
        act = (jax.nn.silu(gate) * up).astype(jnp.bfloat16)
        out = jnp.dot(act, down_proj[0], preferred_element_type=jnp.float32).astype(jnp.bfloat16)
        tiles = retile(out, True)
        return exchange(tiles.reshape(experts, CAP, half)).reshape(slots, half)

    def combine(gates, back):
        sides = jnp.dot(gates, back, preferred_element_type=jnp.float32).reshape(4, rows, half)
        return jnp.concatenate(
            [sides[at] * (1 / 256) + sides[at + 1] * (1 / 65536) for at in (0, 2)], axis=1
        )

    routes = [routing(part) for part in range(PARTS)]
    arrived = [send(pick) for pick, _ in routes]
    returned = [expert(tokens) for tokens in arrived]
    expert_sum = sum(combine(gates, back) for (_, gates), back in zip(routes, returned))
    layer_output = (after_float + expert_sum).astype(jnp.bfloat16)
    return (after_attention[None], layer_output[None])


def solution(mesh):
    tokens = P("exp", "ctx", None)
    experts = P(("ctx", "exp"), None, None)
    return jax.shard_map(
        per_device,
        mesh=mesh,
        in_specs=(tokens,) * 6
        + (P(("ctx", "exp"), None), P(), experts, experts, experts, tokens, tokens),
        out_specs=(tokens, tokens),
        check_vma=False,
    )
```
